32 devices in a mesh: pipe: 4 (over x, core), expert: 4 (over z), pair: 2 (over y).
Axes of the slice: x: 2, y: 2, z: 4, core: 2. Of those that a mesh axis runs over, the one named last changes fastest.
Arguments:
- tokens: bfloat16 [4096, 2048], P(('pipe', 'expert')), may hold values from -8 to 8
- expert_ids: int32 [4096, 2], P(('pipe', 'expert')), may hold values from 0 to 3, all different within a row; in each aligned block of 256 rows (0 to 255, 256 to 511, ...) at most 256 rows name the same one
- block_mask: int32 [32, 8], P(('pipe', 'expert')), may hold values from 0 to 1, as said below
- attn_gain: float32 [4, 2048], P('pipe'), may hold values from 0.1 to 1.9
- w_qkv: bfloat16 [4, 2048, 8, 384], P('pipe', None, 'pair'), may hold values from -3 to 3
- w_out: bfloat16 [4, 8, 128, 2048], P('pipe', 'pair'), may hold values from -4 to 4
- moe_gain: float32 [4, 2048], P('pipe'), may hold values from 0.1 to 1.9
- w_router: bfloat16 [4, 2048, 4], P('pipe'), may hold values from -0.125 to 0.125
- w_up: bfloat16 [4, 4, 2048, 3584], P('pipe', 'expert', None, 'pair'), may hold values from -0.125 to 0.125
- w_down: bfloat16 [4, 4, 3584, 2048], P('pipe', 'expert', 'pair'), may hold values from -0.09375 to 0.09375
Outputs:
- next_input: bfloat16 [4096, 2048], P(('pipe', 'expert'))
The draws below stay inside these ranges and needn't reach their ends.
Inputs may be any that keep to these rules, and one draw needn't show every extreme that they name: `expert_ids`: in each aligned block of 256 rows (the rows of one device) no expert is named by more than 256 rows. `block_mask`: entry [b, c] is 1 where query block b may attend to key block c of its own micro-batch; every block attends to itself.
All inputs are finite; a program needn't handle non-finite values.
Results may differ from the reference program's by a relative error of at most 0.0095.
Values may be sent and summed in bfloat16 or wider, within the bound.
No kernel may reach another device: no remote copies, remote signals or barrier semaphores. Data moves between devices by JAX's collectives and lax.ppermute only.
A program may use at most 128 MiB of HBM per device.

```python
import math
import jax
import jax.numpy as jnp
import numpy as np
from jax import lax

D = 2048
HEADS = 8
HEAD_DIM = 128
FF = 3584
TOP = 2
BLOCK = 128
ROWS = 256
EXPERTS = 4
CAP = 256
MB_TOK = 1024
TOKENS = 4096
N_PIPE = 4
N_EXPERT = 4
N_PAIR = 2


def draw_tokens(key, part):
    first = jax.random.fold_in(key, 0)
    base = jax.random.normal(first, (TOKENS, D), jnp.float32)
    return jnp.clip(base, -8.0, 8.0).astype(jnp.bfloat16)


def draw_w_qkv(key, part):
    first = jax.random.fold_in(key, 0)
    spread = D ** (-0.5)
    base = jnp.clip(jax.random.normal(first, (N_PIPE, D, HEADS, 3 * HEAD_DIM), jnp.float32), -6.0, 6.0) * spread
    return base.astype(jnp.bfloat16)


def draw_block_mask(key, part):
    mask_rows = TOKENS // BLOCK
    mask_cols = MB_TOK // BLOCK
    picked = jax.random.randint(key, (mask_rows, mask_cols), 0, 4)
    itself = jnp.arange(mask_rows, dtype=jnp.int32)[:, None] % mask_cols == jnp.arange(mask_cols, dtype=jnp.int32)[None, :]
    return jnp.where(itself | (picked == 0), 1, 0).astype(jnp.int32)


def levels(key, extent, cuts, smallest, top_value):
    loudness, own = 1.0, jax.random.fold_in(key, 6)
    for axis_at, parts in cuts:
        heights = jnp.exp(jax.random.uniform(jax.random.fold_in(own, axis_at), (parts,), jnp.float32, smallest / len(cuts), top_value / len(cuts)))
        loudness = loudness * jnp.repeat(heights, extent[axis_at] // parts).reshape([-1 if axis == axis_at else 1 for axis in range(len(extent))])
    return loudness


def assign_block(own_key, own, number, rows, number_of, top, limit, lean):
    ranking = jax.random.permutation(own_key, number_of)
    heavy_load, common = portions_of(number_of, rows * top, limit, lean, True), portions_of(number_of, rows * top, limit, lean, False)
    places = jnp.arange(number_of)

    def named(sizes, rotation):
        used = int((sizes > 0).sum())
        fixed = max(1, used // 4)
        passed = fixed + (places - fixed + rotation * (used - fixed)) % max(1, number_of - fixed)
        return jnp.zeros((number_of,), jnp.int32).at[ranking[jnp.where(places < fixed, places, passed)]].set(jnp.asarray(sizes, jnp.int32))

    sizes = jnp.where(number % 4 == 0, named(heavy_load, number // 4), named(common, number - number // 4 - 1))
    mixed = jax.random.permutation(jax.random.fold_in(own, 3), number_of)
    donor, taker = mixed[0:number_of // 2 * 2:2], mixed[1:number_of // 2 * 2:2]
    room = jnp.minimum(sizes[donor] - 1, limit - sizes[taker]) // 2
    room = jnp.where((donor == ranking[0]) | (taker == ranking[0]) | (sizes[taker] == 0), 0, jnp.maximum(room, 0))
    passed = jax.random.randint(jax.random.fold_in(own, 4), (number_of // 2,), 0, 1 << 20) % (room + 1)
    sizes = sizes.at[donor].add(-passed).at[taker].add(passed)
    labels = jnp.searchsorted(jnp.cumsum(sizes), jnp.arange(rows * top), side="right").astype(jnp.int32)
    grid = labels.reshape(top, rows).T
    grid = grid[jax.random.permutation(jax.random.fold_in(own, 1), rows)]
    rotation = jax.random.randint(jax.random.fold_in(own, 2), (rows, 1), 0, top)
    return jnp.take_along_axis(grid, (jnp.arange(top)[None, :] + rotation) % top, axis=1)


def portions_of(count, total, most, lean, full):
    portions = [(1 << 20) // math.isqrt(grade ** lean) + 1 for grade in range(1, count + 1)]
    largest = most if full else min(most, max(-(-total // count), total * portions[0] // sum(portions)))
    least = 1 if total - largest >= count - 1 else 0
    counts, spare = [largest] + [least] * (count - 1), total - largest - least * (count - 1)
    while spare > 0:
        free = [i for i in range(1, count) if counts[i] < largest] or [i for i in range(1, count) if counts[i] < most]
        pool, remaining = sum([portions[i] for i in free]), spare
        for i in free:
            addition = min(most - counts[i], max(1, remaining * portions[i] // pool), spare)
            counts[i] = counts[i] + addition
            spare = spare - addition
    return np.array(counts)


def gaussian(stream_key, shape, scale, bound, shards=(), held_as=jnp.bfloat16):
    level = levels(stream_key, shape, shards, -0.22, 0.18) if shards else 1.0
    entries = jax.random.normal(stream_key, shape, jnp.float32) * scale * level
    return jnp.minimum(jnp.maximum(entries, -bound), bound).astype(held_as)


def setup_inputs(seed: int = 0) -> dict:
    keys = jax.random.split(jax.random.key(seed), 11)
    tokens = draw_tokens(jax.random.fold_in(keys[10], 71), 0)
    expert_ids_keys = jax.random.split(jax.random.fold_in(keys[1], 1), TOKENS // ROWS)
    expert_ids_turns = jax.random.permutation(jax.random.fold_in(keys[1], 3), TOKENS // ROWS)
    expert_ids = jax.vmap(lambda own, number: assign_block(jax.random.fold_in(keys[1], 2), own, number, ROWS, EXPERTS, TOP, CAP, 1))(expert_ids_keys, expert_ids_turns).reshape((TOKENS, TOP))
    block_mask = draw_block_mask(jax.random.fold_in(keys[10], 71), 0)
    attn_gain = jnp.clip(1.0 + 0.18 * jax.random.normal(keys[3], (N_PIPE, D), jnp.float32), 0.1, 1.9)
    w_qkv = draw_w_qkv(jax.random.fold_in(keys[10], 71), 0)
    w_out = gaussian(keys[5], (N_PIPE, HEADS, HEAD_DIM, D), 0.3, 4.0, ((0, 4), (1, 2)))
    moe_gain = jnp.clip(1.0 + 0.18 * jax.random.normal(keys[6], (N_PIPE, D), jnp.float32), 0.1, 1.9)
    w_router = gaussian(keys[7], (N_PIPE, D, EXPERTS), D ** -0.5, 0.125, ((0, 4),))
    w_up = gaussian(keys[8], (N_PIPE, EXPERTS, D, FF), D ** -0.5, 0.125, ((0, 4), (1, 4), (3, 2)))
    w_down = gaussian(keys[9], (N_PIPE, EXPERTS, FF, D), FF ** -0.5, 0.09375, ((0, 4), (1, 4), (2, 2)))
    return dict(tokens=tokens, expert_ids=expert_ids, block_mask=block_mask, attn_gain=attn_gain, w_qkv=w_qkv, w_out=w_out, moe_gain=moe_gain, w_router=w_router, w_up=w_up, w_down=w_down)


def rms_scale(values, gain):
    widened = values.astype(jnp.float32)
    return widened * lax.rsqrt(lax.optimization_barrier(jnp.mean(widened * widened, axis=-1, keepdims=True)) + 1e-05) * gain

def rounded(values):
    return lax.optimization_barrier(values.astype(jnp.bfloat16)).astype(jnp.float32)

def attend(normed, layer_qkv, layer_out_weight, mask_rows):
    projected = jnp.einsum('td,dhc->thc', normed.astype(jnp.float32), layer_qkv.astype(jnp.float32)).astype(jnp.bfloat16)
    queries = projected[:, :, :HEAD_DIM].astype(jnp.float32)
    key_rows = projected[:, :, HEAD_DIM:2 * HEAD_DIM].astype(jnp.float32)
    value_rows = projected[:, :, 2 * HEAD_DIM:].astype(jnp.float32)

    def one_block(block_index):
        query_rows = lax.dynamic_slice_in_dim(queries, block_index * BLOCK, BLOCK, 0)
        scores = jnp.einsum('qhc,khc->hqk', query_rows, key_rows) * HEAD_DIM ** (-0.5)
        allowed = jnp.repeat(mask_rows[block_index], BLOCK) > 0
        masked = jnp.where(allowed, scores, -1e+30)
        row_max = lax.optimization_barrier(jnp.max(masked, axis=-1, keepdims=True))
        weights = jnp.where(allowed, jnp.exp(masked - row_max), 0.0)
        denominator = lax.optimization_barrier(jnp.sum(weights, axis=-1))
        summed = jnp.einsum('hqk,khc->qhc', rounded(weights), value_rows)
        return (summed / jnp.transpose(denominator)[:, :, None]).astype(jnp.bfloat16)
    blocks = MB_TOK // BLOCK
    attended = lax.map(one_block, jnp.arange(blocks, dtype=jnp.int32)).reshape(MB_TOK, HEADS, HEAD_DIM)
    per_group = HEADS // N_PAIR
    partials = jnp.einsum('tghc,ghcd->gtd', attended.reshape(MB_TOK, N_PAIR, per_group, HEAD_DIM).astype(jnp.float32), layer_out_weight.reshape(N_PAIR, per_group, HEAD_DIM, D).astype(jnp.float32))
    return lax.optimization_barrier(jnp.sum(rounded(partials), axis=0))

def experts_out(moe_in, section_ids, layer_up, layer_down):
    copies = MB_TOK * TOP
    flat_ids = section_ids.reshape(copies)
    room_all = N_EXPERT * CAP
    per_group = FF // N_PAIR

    def one_expert(running, expert_index):
        chosen_here = flat_ids == expert_index
        position = jnp.cumsum(chosen_here.astype(jnp.int32)) - 1
        target = jnp.where(chosen_here, position, room_all)
        source_copy = jnp.zeros((room_all,), jnp.int32).at[target].set(jnp.arange(copies, dtype=jnp.int32), mode='drop')
        gathered = jnp.take(moe_in, source_copy // TOP, axis=0)
        lifted = jnp.dot(gathered, layer_up[expert_index], preferred_element_type=jnp.float32)
        hidden = jax.nn.gelu(lifted, approximate=True).astype(jnp.bfloat16)
        partials = jnp.einsum('rgf,gfd->grd', hidden.reshape(room_all, N_PAIR, per_group).astype(jnp.float32), layer_down[expert_index].reshape(N_PAIR, per_group, D).astype(jnp.float32))
        result = rounded(lax.optimization_barrier(jnp.sum(rounded(partials), axis=0)))
        picked = jnp.take(result, jnp.clip(position, 0, room_all - 1), axis=0)
        return (running + jnp.where(chosen_here[:, None], picked, 0.0), None)
    running = lax.scan(one_expert, jnp.zeros((copies, D), jnp.float32), jnp.arange(EXPERTS, dtype=jnp.int32))[0]
    return running.reshape(MB_TOK, TOP, D)

def reference(tokens, expert_ids, block_mask, attn_gain, w_qkv, w_out, moe_gain, w_router, w_up, w_down):
    blocks = MB_TOK // BLOCK
    results = []
    for section in range(N_PIPE):
        stream = tokens[section * MB_TOK:(section + 1) * MB_TOK]
        section_ids = expert_ids[section * MB_TOK:(section + 1) * MB_TOK]
        mask_rows = block_mask[section * blocks:(section + 1) * blocks]
        normed = rms_scale(stream, attn_gain[section]).astype(jnp.bfloat16)
        residual = stream.astype(jnp.float32) + attend(normed, w_qkv[section], w_out[section], mask_rows)
        moe_in = rms_scale(residual, moe_gain[section]).astype(jnp.bfloat16)
        logits = jnp.dot(moe_in, w_router[section], preferred_element_type=jnp.float32)
        chosen = jnp.take_along_axis(logits, section_ids, axis=1)
        gate_values = jax.nn.sigmoid(chosen)
        mix_weights = gate_values / lax.optimization_barrier(jnp.sum(gate_values, axis=1, keepdims=True))
        outputs = experts_out(moe_in, section_ids, w_up[section], w_down[section])
        layer_out = residual + lax.optimization_barrier(jnp.sum(mix_weights[:, :, None] * outputs, axis=1))
        results.append(layer_out.astype(jnp.bfloat16))
    return jnp.concatenate([results[-1]] + results[:-1], axis=0)
```

```python
import functools

import jax
import jax.numpy as jnp
from jax import lax
from jax.experimental import pallas as pl
from jax.experimental.pallas import tpu as pltpu
from jax.sharding import PartitionSpec as P

BLOCK = 128


def passed_along(value, axis, steps):
    count = lax.axis_size(axis)
    pairs = [(source, (source + steps) % count) for source in range(count)]
    return lax.ppermute(value, axis, pairs)


def rms_scale(values, gain):
    widened = values.astype(jnp.float32)
    return widened * lax.rsqrt(jnp.mean(widened * widened, axis=-1, keepdims=True) + 1e-05) * gain


def pair_total(partial_term):
    return lax.psum(partial_term.astype(jnp.bfloat16), "pair").astype(jnp.float32)


def dispatched(
    tokens, expert_ids, block_mask, attn_gain, w_qkv, w_out, moe_gain, w_router, w_up, w_down
):
    rows_here = tokens.shape[0]
    model_width = tokens.shape[1]
    heads_here = w_qkv.shape[2]
    head_dim = w_qkv.shape[3] // 3
    block_count = block_mask.shape[1]
    normed = rms_scale(tokens, attn_gain[0]).astype(jnp.bfloat16)
    projected = jnp.einsum(
        "td,dhc->thc", normed, w_qkv[0], preferred_element_type=jnp.float32
    ).astype(jnp.bfloat16)
    queries = projected[:, :, :head_dim]
    key_rows = projected[:, :, head_dim : 2 * head_dim]
    value_rows = projected[:, :, 2 * head_dim :]
    mask_local = block_mask.astype(jnp.float32)
    score_scale = head_dim ** (-0.5)
    start_max = jnp.full((heads_here, rows_here), -1e30, jnp.float32)
    row_max = start_max
    shard_keys = lax.all_gather(key_rows, "expert", axis=0, tiled=True)
    shard_values = lax.all_gather(value_rows, "expert", axis=0, tiled=True)
    shard_rows = shard_keys.shape[0]
    scores = (
        jnp.einsum("qhc,khc->hqk", queries, shard_keys, preferred_element_type=jnp.float32)
        * score_scale
    )
    key_block = jnp.arange(shard_rows, dtype=jnp.int32) // BLOCK
    selector = (key_block[:, None] == jnp.arange(block_count, dtype=jnp.int32)[None, :]).astype(
        jnp.float32
    )
    allowed_blocks = jnp.dot(mask_local, jnp.transpose(selector))
    allowed = jnp.repeat(allowed_blocks, BLOCK, axis=0)[None] > 0.5
    masked = jnp.where(allowed, scores, -1e30)
    new_max = jnp.maximum(row_max, jnp.max(masked, axis=-1))
    weights = jnp.where(allowed, jnp.exp(masked - new_max[:, :, None]), 0.0)
    denominator = jnp.sum(weights, axis=-1)
    numerator = jnp.einsum(
        "hqk,khc->qhc",
        weights.astype(jnp.bfloat16),
        shard_values,
        preferred_element_type=jnp.float32,
    )
    row_max, denominator, numerator = (new_max, denominator, numerator)
    attended = (numerator / jnp.transpose(denominator)[:, :, None]).astype(jnp.bfloat16)
    mixed = jnp.einsum("thc,hcd->td", attended, w_out[0], preferred_element_type=jnp.float32)
    residual = tokens.astype(jnp.float32) + pair_total(mixed)
    moe_in = rms_scale(residual, moe_gain[0]).astype(jnp.bfloat16)
    logits = jnp.dot(moe_in, w_router[0], preferred_element_type=jnp.float32)
    expert_count = logits.shape[1]
    picks_top = expert_ids.shape[1]
    one_hot = expert_ids[:, :, None] == jnp.arange(expert_count, dtype=jnp.int32)[None, None, :]
    chosen = jnp.sum(jnp.where(one_hot, logits[:, None, :], 0.0), axis=-1)
    gate_values = jax.nn.sigmoid(chosen)
    mix_weights = gate_values / jnp.sum(gate_values, axis=1, keepdims=True)
    copy_hits = one_hot.reshape(rows_here * picks_top, expert_count).astype(jnp.int32)
    position = jnp.sum((jnp.cumsum(copy_hits, axis=0) - 1) * copy_hits, axis=1)
    counts = jnp.sum(copy_hits, axis=0)
    capacity = min(rows_here, 2 * rows_here * picks_top // expert_count)
    flat_slot = expert_ids.reshape(-1) * capacity + position
    source_copy = (
        jnp.zeros((expert_count * capacity,), jnp.int32)
        .at[flat_slot]
        .set(jnp.arange(1, rows_here * picks_top + 1, dtype=jnp.int32))
    )
    filled = source_copy > 0
    taken = jnp.take(moe_in, jnp.maximum(source_copy - 1, 0) // picks_top, axis=0)
    outgoing = jnp.where(filled[:, None], taken, jnp.zeros((), jnp.bfloat16)).reshape(
        expert_count, capacity, model_width
    )
    count_column = counts.reshape(expert_count, 1)
    arrived, arrived_counts = (
        lax.all_to_all(outgoing, "expert", split_axis=0, concat_axis=0, tiled=True),
        lax.all_to_all(count_column, "expert", split_axis=0, concat_axis=0, tiled=True),
    )
    sources = arrived.shape[0]
    slot_total = sources * capacity
    flat_rows = arrived.reshape(slot_total, model_width)
    up_weight = w_up[0, 0]
    down_weight = w_down[0, 0]
    lifted = jnp.dot(flat_rows, up_weight, preferred_element_type=jnp.float32)
    hidden = jax.nn.gelu(lifted, approximate=True).astype(jnp.bfloat16)
    partial_out = jnp.dot(hidden, down_weight, preferred_element_type=jnp.float32)
    partial_out = partial_out.reshape(sources, capacity, model_width)
    summed = pair_total(partial_out).astype(jnp.bfloat16)
    back = lax.all_to_all(summed, "expert", split_axis=0, concat_axis=0, tiled=True)
    back_rows = back.reshape(expert_count * capacity, model_width)
    returned = jnp.take(back_rows, flat_slot, axis=0).reshape(rows_here, picks_top, model_width)
    layer_out = (
        residual + jnp.sum(mix_weights[:, :, None] * returned.astype(jnp.float32), axis=1)
    ).astype(jnp.bfloat16)
    return passed_along(layer_out, "pipe", 1)


def swapped(value, axis, bit):
    count = lax.axis_size(axis)
    return lax.ppermute(value, axis, [(source, source ^ bit) for source in range(count)])


def attention_kernel(mask_ref, query_ref, *refs, shards, score_scale):
    kv_refs, out_ref = refs[:shards], refs[shards]
    rows, head_dim = query_ref.shape[1], query_ref.shape[2]
    blocks_here = rows // BLOCK
    shard_blocks = kv_refs[0].shape[1] // BLOCK
    for block in range(blocks_here):
        queries = query_ref[0, block * BLOCK : (block + 1) * BLOCK, :]
        masked, flags = [], []
        for shard in range(shards):
            keys = kv_refs[shard][0, :, :head_dim]
            scores = lax.dot_general(
                queries, keys, (((1,), (1,)), ((), ())), preferred_element_type=jnp.float32
            )
            scores = scores * score_scale
            for part in range(shard_blocks):
                flag = mask_ref[block, shard * shard_blocks + part] > 0
                piece = scores[:, part * BLOCK : (part + 1) * BLOCK]
                masked.append(jnp.where(flag, piece, -1e30))
                flags.append(flag)
        tallest = functools.reduce(jnp.maximum, masked)
        row_max = jnp.max(tallest, axis=-1, keepdims=True)
        weights = [
            jnp.where(flag, jnp.exp(piece - row_max), 0.0) for flag, piece in zip(flags, masked)
        ]
        denominator = jnp.sum(functools.reduce(jnp.add, weights), axis=-1, keepdims=True)
        numerator = jnp.zeros((BLOCK, head_dim), jnp.float32)
        for shard in range(shards):
            pieces = weights[shard * shard_blocks : (shard + 1) * shard_blocks]
            joined = jnp.concatenate(pieces, axis=1).astype(jnp.bfloat16)
            numerator = numerator + jnp.dot(
                joined, kv_refs[shard][0, :, head_dim:], preferred_element_type=jnp.float32
            )
        attended = (numerator / denominator).astype(jnp.bfloat16)
        out_ref[block * BLOCK : (block + 1) * BLOCK, :] = attended


def attention(mask, queries, kv_shards):
    heads, rows, head_dim = queries.shape
    shards = len(kv_shards)
    kernel = functools.partial(attention_kernel, shards=shards, score_scale=head_dim ** (-0.5))
    kv_spec = pl.BlockSpec((1, rows, 2 * head_dim), lambda head, mask_ref: (head, 0, 0))
    return pl.pallas_call(
        kernel,
        out_shape=jax.ShapeDtypeStruct((rows, heads * head_dim), jnp.bfloat16),
        grid_spec=pltpu.PrefetchScalarGridSpec(
            num_scalar_prefetch=1,
            grid=(heads,),
            in_specs=[pl.BlockSpec((1, rows, head_dim), lambda head, mask_ref: (head, 0, 0))]
            + [kv_spec] * shards,
            out_specs=pl.BlockSpec((rows, head_dim), lambda head, mask_ref: (0, head)),
        ),
    )(mask, queries, *kv_shards)


def expert_kernel(kept_ref, given_ref, kept_mix_ref, given_mix_ref, up_ref, down_ref,
                  kept_out_ref, given_out_ref, total_ref):
    step = pl.program_id(0)
    half = kept_ref.shape[0]
    rows = jnp.concatenate([kept_ref[...], given_ref[...]], axis=0)
    lifted = jnp.dot(rows, up_ref[...], preferred_element_type=jnp.float32)
    hidden = jax.nn.gelu(lifted, approximate=True).astype(jnp.bfloat16)
    partial_out = jnp.dot(hidden, down_ref[...], preferred_element_type=jnp.float32)

    @pl.when(step == 0)
    def _():
        total_ref[...] = partial_out

    @pl.when(step > 0)
    def _():
        total_ref[...] += partial_out

    @pl.when(step == pl.num_programs(0) - 1)
    def _():
        kept_out_ref[...] = (total_ref[:half] * kept_mix_ref[...]).astype(jnp.bfloat16)
        given_out_ref[...] = (total_ref[half:] * given_mix_ref[...]).astype(jnp.bfloat16)


def largest_tile(extent, most):
    return max(tile for tile in range(128, most + 1, 128) if extent % tile == 0)


def expert_parts(kept, given, kept_mix, given_mix, up_weight, down_weight):
    half, width = kept.shape
    hidden_units = up_weight.shape[1]
    tile = largest_tile(hidden_units, 512)
    whole_rows = pl.BlockSpec((half, width), lambda step: (0, 0))
    whole_mix = pl.BlockSpec((half, 1), lambda step: (0, 0))
    out = jax.ShapeDtypeStruct((half, width), jnp.bfloat16)
    return pl.pallas_call(
        expert_kernel,
        out_shape=(out, out),
        grid=(hidden_units // tile,),
        in_specs=[
            whole_rows,
            whole_rows,
            whole_mix,
            whole_mix,
            pl.BlockSpec((width, tile), lambda step: (0, step)),
            pl.BlockSpec((tile, width), lambda step: (step, 0)),
        ],
        out_specs=(whole_rows, whole_rows),
        scratch_shapes=[pltpu.VMEM((2 * half, width), jnp.float32)],
    )(kept, given, kept_mix, given_mix, up_weight, down_weight)


def gathered(
    tokens, expert_ids, block_mask, attn_gain, w_qkv, w_out, moe_gain, w_router, w_up, w_down
):
    rows_here, model_width = tokens.shape
    head_dim = w_qkv.shape[3] // 3
    experts = lax.axis_size("expert")
    here = lax.axis_index("expert")
    side = lax.axis_index("pair")
    half = rows_here // 2
    own_out = w_out[0].reshape(-1, model_width)
    other_out = swapped(own_out, "pair", 1)

    normed = rms_scale(tokens, attn_gain[0]).astype(jnp.bfloat16)
    kv_own = jnp.einsum(
        "td,dhc->htc", normed, w_qkv[0, :, :, head_dim:], preferred_element_type=jnp.float32
    ).astype(jnp.bfloat16)
    queries = jnp.einsum(
        "td,dhc->htc", normed, w_qkv[0, :, :, :head_dim], preferred_element_type=jnp.float32
    ).astype(jnp.bfloat16)
    kv_shards = [kv_own] + [swapped(kv_own, "expert", bit) for bit in range(1, experts)]
    blocks_here = rows_here // BLOCK
    mask = jnp.concatenate(
        [
            lax.dynamic_slice_in_dim(block_mask, (here ^ bit) * blocks_here, blocks_here, 1)
            for bit in range(experts)
        ],
        axis=1,
    )
    attended = attention(mask, queries, kv_shards)
    other_attended = swapped(attended, "pair", 1)

    def mixed(part, weight):
        total = jnp.dot(part, weight, preferred_element_type=jnp.float32)
        return total.astype(jnp.bfloat16).astype(jnp.float32)

    residual = tokens.astype(jnp.float32) + (
        mixed(attended, own_out) + mixed(other_attended, other_out)
    )
    moe_in = rms_scale(residual, moe_gain[0]).astype(jnp.bfloat16)
    logits = jnp.dot(moe_in, w_router[0], preferred_element_type=jnp.float32)
    expert_index = jnp.arange(logits.shape[1], dtype=jnp.int32)
    one_hot = expert_ids[:, :, None] == expert_index[None, None, :]
    chosen = jnp.sum(jnp.where(one_hot, logits[:, None, :], 0.0), axis=-1)
    gate_values = jax.nn.sigmoid(chosen)
    mix_weights = gate_values / jnp.sum(gate_values, axis=1, keepdims=True)
    spread_mix = jnp.sum(jnp.where(one_hot, mix_weights[:, :, None], 0.0), axis=1)

    def kept_half(value):
        return lax.dynamic_slice_in_dim(value, side * half, half, 0)

    def given_half(value):
        return lax.dynamic_slice_in_dim(value, (1 - side) * half, half, 0)

    kept_rows = kept_half(moe_in)
    rows = {0: (kept_rows, given_half(moe_in))}
    mix = {0: lax.dynamic_index_in_dim(spread_mix, here, 1, keepdims=False)}
    for bit in range(1, experts):
        brought = swapped(kept_rows, "expert", bit)
        rows[bit] = (brought, swapped(brought, "pair", 1))
        column = lax.dynamic_index_in_dim(spread_mix, here ^ bit, 1, keepdims=False)
        mix[bit] = swapped(column, "expert", bit)
    total = kept_half(residual)
    for bit in range(experts):
        column = mix[bit][:, None]
        kept, given = expert_parts(
            *rows[bit], kept_half(column), given_half(column), w_up[0, 0], w_down[0, 0]
        )
        summed = kept.astype(jnp.float32) + swapped(given, "pair", 1).astype(jnp.float32)
        if bit:
            summed = swapped(summed.astype(jnp.bfloat16), "expert", bit).astype(jnp.float32)
        total = total + summed
    layer_out = total.astype(jnp.bfloat16)
    stages, sides = lax.axis_size("pipe"), lax.axis_size("pair")

    def to_next(flip):
        pairs = [
            (stage * sides + place, (stage + 1) % stages * sides + (place ^ flip))
            for stage in range(stages)
            for place in range(sides)
        ]
        return lax.ppermute(layer_out, ("pipe", "pair"), pairs)

    straight, crossed = to_next(0), to_next(1)
    first = jnp.where(side == 0, straight, crossed)
    second = jnp.where(side == 0, crossed, straight)
    return jnp.concatenate([first, second], axis=0)


def local(tokens, expert_ids, block_mask, attn_gain, w_qkv, w_out, moe_gain, w_router, w_up, w_down):
    rows_here = tokens.shape[0]
    experts = lax.axis_size("expert")
    capacity = min(rows_here, 2 * rows_here * expert_ids.shape[1] // experts)
    gathers = capacity == rows_here and lax.axis_size("pair") == 2 and experts & (experts - 1) == 0
    step = gathered if gathers else dispatched
    return step(
        tokens, expert_ids, block_mask, attn_gain, w_qkv, w_out, moe_gain, w_router, w_up, w_down
    )


def solution(mesh):
    return jax.shard_map(
        local,
        mesh=mesh,
        in_specs=(
            P(("pipe", "expert"), None),
            P(("pipe", "expert"), None),
            P(("pipe", "expert"), None),
            P("pipe", None),
            P("pipe", None, "pair", None),
            P("pipe", "pair", None, None),
            P("pipe", None),
            P("pipe", None, None),
            P("pipe", "expert", None, "pair"),
            P("pipe", "expert", "pair", None),
        ),
        out_specs=P(("pipe", "expert"), None),
        check_vma=False,
    )
```

```python
import functools

import jax
import jax.numpy as jnp
from jax import lax
from jax.experimental import pallas as pl
from jax.experimental.pallas import tpu as pltpu
from jax.sharding import PartitionSpec as P


BLOCK = 128
GROUPS = 2
SMALL_VMEM = 2 << 20
LARGE_VMEM = 24 << 20


def passed_along(value, axis, steps):
    count = lax.axis_size(axis)
    pairs = [(source, (source + steps) % count) for source in range(count)]
    return lax.ppermute(value, axis, pairs)


def rms_scale(values, gain):
    widened = values.astype(jnp.float32)
    return widened * lax.rsqrt(jnp.mean(widened * widened, axis=-1, keepdims=True) + 1e-05) * gain


def pair_total(partial_term):
    return lax.psum(partial_term.astype(jnp.bfloat16), "pair").astype(jnp.float32)


def dispatched(
    tokens, expert_ids, block_mask, attn_gain, w_qkv, w_out, moe_gain, w_router, w_up, w_down
):
    rows_here = tokens.shape[0]
    model_width = tokens.shape[1]
    heads_here = w_qkv.shape[2]
    head_dim = w_qkv.shape[3] // 3
    block_count = block_mask.shape[1]
    normed = rms_scale(tokens, attn_gain[0]).astype(jnp.bfloat16)
    projected = jnp.einsum(
        "td,dhc->thc", normed, w_qkv[0], preferred_element_type=jnp.float32
    ).astype(jnp.bfloat16)
    queries = projected[:, :, :head_dim]
    key_rows = projected[:, :, head_dim : 2 * head_dim]
    value_rows = projected[:, :, 2 * head_dim :]
    mask_local = block_mask.astype(jnp.float32)
    score_scale = head_dim ** (-0.5)
    start_max = jnp.full((heads_here, rows_here), -1e30, jnp.float32)
    row_max = start_max
    shard_keys = lax.all_gather(key_rows, "expert", axis=0, tiled=True)
    shard_values = lax.all_gather(value_rows, "expert", axis=0, tiled=True)
    shard_rows = shard_keys.shape[0]
    scores = (
        jnp.einsum("qhc,khc->hqk", queries, shard_keys, preferred_element_type=jnp.float32)
        * score_scale
    )
    key_block = jnp.arange(shard_rows, dtype=jnp.int32) // BLOCK
    selector = (key_block[:, None] == jnp.arange(block_count, dtype=jnp.int32)[None, :]).astype(
        jnp.float32
    )
    allowed_blocks = jnp.dot(mask_local, jnp.transpose(selector))
    allowed = jnp.repeat(allowed_blocks, BLOCK, axis=0)[None] > 0.5
    masked = jnp.where(allowed, scores, -1e30)
    new_max = jnp.maximum(row_max, jnp.max(masked, axis=-1))
    weights = jnp.where(allowed, jnp.exp(masked - new_max[:, :, None]), 0.0)
    denominator = jnp.sum(weights, axis=-1)
    numerator = jnp.einsum(
        "hqk,khc->qhc",
        weights.astype(jnp.bfloat16),
        shard_values,
        preferred_element_type=jnp.float32,
    )
    row_max, denominator, numerator = (new_max, denominator, numerator)
    attended = (numerator / jnp.transpose(denominator)[:, :, None]).astype(jnp.bfloat16)
    mixed = jnp.einsum("thc,hcd->td", attended, w_out[0], preferred_element_type=jnp.float32)
    residual = tokens.astype(jnp.float32) + pair_total(mixed)
    moe_in = rms_scale(residual, moe_gain[0]).astype(jnp.bfloat16)
    logits = jnp.dot(moe_in, w_router[0], preferred_element_type=jnp.float32)
    expert_count = logits.shape[1]
    picks_top = expert_ids.shape[1]
    one_hot = expert_ids[:, :, None] == jnp.arange(expert_count, dtype=jnp.int32)[None, None, :]
    chosen = jnp.sum(jnp.where(one_hot, logits[:, None, :], 0.0), axis=-1)
    gate_values = jax.nn.sigmoid(chosen)
    mix_weights = gate_values / jnp.sum(gate_values, axis=1, keepdims=True)
    copy_hits = one_hot.reshape(rows_here * picks_top, expert_count).astype(jnp.int32)
    position = jnp.sum((jnp.cumsum(copy_hits, axis=0) - 1) * copy_hits, axis=1)
    counts = jnp.sum(copy_hits, axis=0)
    capacity = min(rows_here, 2 * rows_here * picks_top // expert_count)
    flat_slot = expert_ids.reshape(-1) * capacity + position
    source_copy = (
        jnp.zeros((expert_count * capacity,), jnp.int32)
        .at[flat_slot]
        .set(jnp.arange(1, rows_here * picks_top + 1, dtype=jnp.int32))
    )
    filled = source_copy > 0
    taken = jnp.take(moe_in, jnp.maximum(source_copy - 1, 0) // picks_top, axis=0)
    outgoing = jnp.where(filled[:, None], taken, jnp.zeros((), jnp.bfloat16)).reshape(
        expert_count, capacity, model_width
    )
    count_column = counts.reshape(expert_count, 1)
    arrived, arrived_counts = (
        lax.all_to_all(outgoing, "expert", split_axis=0, concat_axis=0, tiled=True),
        lax.all_to_all(count_column, "expert", split_axis=0, concat_axis=0, tiled=True),
    )
    sources = arrived.shape[0]
    slot_total = sources * capacity
    flat_rows = arrived.reshape(slot_total, model_width)
    up_weight = w_up[0, 0]
    down_weight = w_down[0, 0]
    lifted = jnp.dot(flat_rows, up_weight, preferred_element_type=jnp.float32)
    hidden = jax.nn.gelu(lifted, approximate=True).astype(jnp.bfloat16)
    partial_out = jnp.dot(hidden, down_weight, preferred_element_type=jnp.float32)
    partial_out = partial_out.reshape(sources, capacity, model_width)
    summed = pair_total(partial_out).astype(jnp.bfloat16)
    back = lax.all_to_all(summed, "expert", split_axis=0, concat_axis=0, tiled=True)
    back_rows = back.reshape(expert_count * capacity, model_width)
    returned = jnp.take(back_rows, flat_slot, axis=0).reshape(rows_here, picks_top, model_width)
    layer_out = (
        residual + jnp.sum(mix_weights[:, :, None] * returned.astype(jnp.float32), axis=1)
    ).astype(jnp.bfloat16)
    return passed_along(layer_out, "pipe", 1)


def swapped(value, axis, bit):
    count = lax.axis_size(axis)
    return lax.ppermute(value, axis, [(source, source ^ bit) for source in range(count)])


def doubled(own, axis, skip=0):
    slots = [own]
    for slot in range(1, lax.axis_size(axis)):
        if slot <= skip:
            slots.append(None)
        else:
            slots.append(swapped(slots[slot & (slot - 1)], axis, slot & -slot))
    return slots


def held(value):
    parts = 4
    rows = value.shape[0] // parts

    def kernel(source_ref, held_ref, sem):
        copies = []
        for part in range(parts):
            place = pl.ds(part * rows, rows)
            copies.append(
                pltpu.make_async_copy(source_ref.at[place], held_ref.at[place], sem.at[part])
            )
        for copy in copies:
            copy.start()
        for copy in copies:
            copy.wait()

    return pl.pallas_call(
        kernel,
        out_shape=pltpu.VMEM(value.shape, value.dtype),
        in_specs=[pl.BlockSpec(memory_space=pl.ANY)],
        out_specs=pl.BlockSpec(memory_space=pltpu.VMEM),
        scratch_shapes=[pltpu.SemaphoreType.DMA((parts,))],
        compiler_params=pltpu.CompilerParams(vmem_limit_bytes=SMALL_VMEM),
    )(value)


def attention_kernel(index_ref, mask_ref, query_ref, *refs, score_scale):
    kv_refs, out_ref = refs[:-1], refs[-1]
    heads, rows, head_dim = query_ref.shape
    shard_blocks = rows // BLOCK
    for head in range(heads):
        every = []
        for kv_ref in kv_refs:
            scores = lax.dot_general(
                query_ref[head],
                kv_ref[head, :, :head_dim],
                (((1,), (1,)), ((), ())),
                preferred_element_type=jnp.float32,
            )
            every.append(scores * score_scale)
        for block in range(rows // BLOCK):
            span = slice(block * BLOCK, (block + 1) * BLOCK)
            masked, flags = [], []
            for shard, scores in enumerate(every):
                for part in range(shard_blocks):
                    flag = mask_ref[block, (index_ref[0] ^ shard) * shard_blocks + part] > 0
                    piece = scores[span, part * BLOCK : (part + 1) * BLOCK]
                    masked.append(jnp.where(flag, piece, -1e30))
                    flags.append(flag)
            tallest = functools.reduce(jnp.maximum, masked)
            row_max = jnp.max(tallest, axis=-1, keepdims=True)
            weights = [
                jnp.where(flag, jnp.exp(piece - row_max), 0.0)
                for flag, piece in zip(flags, masked)
            ]
            denominator = jnp.sum(functools.reduce(jnp.add, weights), axis=-1, keepdims=True)
            numerator = jnp.zeros((BLOCK, head_dim), jnp.float32)
            for shard, kv_ref in enumerate(kv_refs):
                pieces = weights[shard * shard_blocks : (shard + 1) * shard_blocks]
                joined = jnp.concatenate(pieces, axis=1).astype(jnp.bfloat16)
                numerator = numerator + jnp.dot(
                    joined, kv_ref[head, :, head_dim:], preferred_element_type=jnp.float32
                )
            attended = (numerator / denominator).astype(jnp.bfloat16)
            out_ref[span, head * head_dim : (head + 1) * head_dim] = attended


def attention(group, index, mask, queries, kv_own, kv_others):
    heads, rows, kv_width = kv_others[0].shape
    head_dim = queries.shape[2]
    whole_kv = pl.BlockSpec((heads, rows, kv_width), lambda step, *_: (0, 0, 0))
    return pl.pallas_call(
        functools.partial(attention_kernel, score_scale=head_dim ** (-0.5)),
        out_shape=jax.ShapeDtypeStruct((rows, heads * head_dim), jnp.bfloat16),
        grid_spec=pltpu.PrefetchScalarGridSpec(
            num_scalar_prefetch=2,
            grid=(1,),
            in_specs=[
                pl.BlockSpec((heads, rows, head_dim), lambda step, *_: (group, 0, 0)),
                pl.BlockSpec((heads, rows, kv_width), lambda step, *_: (group, 0, 0)),
            ]
            + [whole_kv] * len(kv_others),
            out_specs=pl.BlockSpec((rows, heads * head_dim), lambda step, *_: (0, 0)),
        ),
        compiler_params=pltpu.CompilerParams(vmem_limit_bytes=LARGE_VMEM),
    )(index, mask, queries, kv_own, *kv_others)


def blend_kernel(index_ref, *refs, groups, kept):
    own_refs, other_refs = refs[:groups], refs[groups : 2 * groups]
    own_out_ref, other_out_ref, stream_ref, gain_ref = refs[2 * groups : 2 * groups + 4]
    outs = refs[2 * groups + 4 :]
    half, _ = outs[0].shape
    side = index_ref[1] if kept else 1 - index_ref[1]
    rows = pl.ds(pl.multiple_of(side * half, half), half)

    def mixed(part_refs, weight_ref):
        part = jnp.concatenate([part_ref[rows, :] for part_ref in part_refs], axis=1)
        total = jnp.dot(part, weight_ref[...], preferred_element_type=jnp.float32)
        return total.astype(jnp.bfloat16).astype(jnp.float32)

    both = mixed(own_refs, own_out_ref) + mixed(other_refs, other_out_ref)
    residual = stream_ref[rows, :].astype(jnp.float32) + both
    normed = rms_scale(residual, gain_ref[...]).astype(jnp.bfloat16)
    outs[0][...] = normed
    if kept:
        quarter = half // 2
        outs[1][...] = normed[:quarter]
        outs[2][...] = normed[quarter:]
        outs[3][...] = residual


def blend(index, own_parts, other_parts, own_out, other_out, tokens, gain, kept):
    rows, model_width = tokens.shape
    half = rows // 2
    whole = jax.ShapeDtypeStruct((half, model_width), jnp.bfloat16)
    part = jax.ShapeDtypeStruct((half // 2, model_width), jnp.bfloat16)
    residual = jax.ShapeDtypeStruct((half, model_width), jnp.float32)
    out_shape = (whole, part, part, residual) if kept else (whole,)
    here = pl.BlockSpec(memory_space=pltpu.VMEM)

    def full(value):
        return pl.BlockSpec(value.shape, lambda step, index_ref: (0,) * len(value.shape))

    moved = [*own_parts, *other_parts]
    return pl.pallas_call(
        functools.partial(blend_kernel, groups=len(own_parts), kept=kept),
        out_shape=out_shape,
        grid_spec=pltpu.PrefetchScalarGridSpec(
            num_scalar_prefetch=1,
            grid=(1,),
            in_specs=[full(value) for value in moved] + [here, here, full(tokens), full(gain)],
            out_specs=tuple(full(value) for value in out_shape),
        ),
        compiler_params=pltpu.CompilerParams(vmem_limit_bytes=LARGE_VMEM),
    )(index, *moved, own_out, other_out, tokens, gain)


def largest_tile(extent, most):
    return max(tile for tile in range(128, most + 1, 128) if extent % tile == 0)


def expert_kernel(*refs, pieces):
    piece_refs = refs[:pieces]
    up_ref, down_ref, kept_out_ref, given_out_ref, hidden_ref = refs[pieces:]
    half, width = kept_out_ref.shape
    hidden_units = up_ref.shape[1]
    rows = jnp.concatenate([piece_ref[...] for piece_ref in piece_refs], axis=0)
    tile = largest_tile(hidden_units, 1024)
    for start in range(0, hidden_units, tile):
        lifted = jnp.dot(
            rows, up_ref[:, start : start + tile], preferred_element_type=jnp.float32
        )
        hidden = jax.nn.gelu(lifted, approximate=True).astype(jnp.bfloat16)
        hidden_ref[:, start : start + tile] = hidden
    tile = largest_tile(width, 512)
    for start in range(0, width, tile):
        partial_out = jnp.dot(
            hidden_ref[...], down_ref[:, start : start + tile], preferred_element_type=jnp.float32
        ).astype(jnp.bfloat16)
        kept_out_ref[:, start : start + tile] = partial_out[:half]
        given_out_ref[:, start : start + tile] = partial_out[half:]


def expert_parts(kept, given, up_weight, down_weight):
    rows = list(kept) + list(given)
    half = sum(piece.shape[0] for piece in kept)
    width, hidden_units = up_weight.shape
    out = jax.ShapeDtypeStruct((half, width), jnp.bfloat16)
    here = pl.BlockSpec(memory_space=pltpu.VMEM)
    return pl.pallas_call(
        functools.partial(expert_kernel, pieces=len(rows)),
        out_shape=(out, out),
        grid=(1,),
        in_specs=[pl.BlockSpec(piece.shape, lambda step: (0, 0)) for piece in rows] + [here] * 2,
        out_specs=(pl.BlockSpec((half, width), lambda step: (0, 0)),) * 2,
        scratch_shapes=[pltpu.VMEM((2 * half, hidden_units), jnp.bfloat16)],
        compiler_params=pltpu.CompilerParams(vmem_limit_bytes=LARGE_VMEM),
    )(*rows, up_weight, down_weight)


def gathered(
    tokens, expert_ids, block_mask, attn_gain, w_qkv, w_out, moe_gain, w_router, w_up, w_down
):
    return section_step(
        tokens,
        expert_ids,
        block_mask,
        attn_gain,
        w_qkv,
        w_out,
        moe_gain,
        w_router,
        w_up,
        w_down,
    )


def section_step(
    tokens, expert_ids, block_mask, attn_gain, w_qkv, w_out, moe_gain, w_router, w_up, w_down
):
    rows_here, model_width = tokens.shape
    head_dim = w_qkv.shape[3] // 3
    experts = lax.axis_size("expert")
    here = lax.axis_index("expert")
    side = lax.axis_index("pair")
    half = rows_here // 2
    group_heads = w_qkv.shape[2] // GROUPS

    other_out = swapped(w_out[0].reshape(-1, model_width), "pair", 1)
    normed = rms_scale(tokens, attn_gain[0]).astype(jnp.bfloat16)

    def project(first, last):
        weight = w_qkv[0, :, :, first * head_dim : last * head_dim]
        total = jnp.einsum("td,dhc->htc", normed, weight, preferred_element_type=jnp.float32)
        return total.astype(jnp.bfloat16)

    kv_own = project(1, 3)
    kv_slots = [
        doubled(kv_own[group * group_heads : (group + 1) * group_heads], "expert")
        for group in range(GROUPS)
    ]
    queries = project(0, 1)
    expert_index = jnp.arange(experts, dtype=jnp.int32)
    one_hot = lax.dynamic_slice_in_dim(expert_ids, side * half, half, 0)[:, :, None] == expert_index
    slot_here = (expert_index[:, None] ^ here == expert_index).astype(jnp.float32)
    index = jnp.stack([here, side])
    up_weight, one_hot, slot_here, index = lax.optimization_barrier(
        (w_up[0, 0], one_hot.astype(jnp.float32), slot_here, index)
    )
    up_held = held(up_weight)
    down_held = held(w_down[0, 0])
    attended, other_attended = [], []
    for group in range(GROUPS):
        attended.append(attention(group, index, block_mask, queries, kv_own, kv_slots[group][1:]))
        other_attended.append(swapped(attended[group], "pair", 1))
    own_held = held(w_out[0].reshape(-1, model_width))
    other_held = held(other_out)

    def blended(kept):
        return blend(index, attended, other_attended, own_held, other_held, tokens, moe_gain, kept)

    kept_rows, upper_rows, lower_rows, residual = blended(True)
    (given_rows,) = blended(False)

    logits = jnp.dot(kept_rows, w_router[0], preferred_element_type=jnp.float32)
    chosen = jnp.sum(one_hot * logits[:, None, :], axis=-1)
    gate_values = jax.nn.sigmoid(chosen)
    mix_weights = gate_values / jnp.sum(gate_values, axis=1, keepdims=True)
    spread_mix = jnp.sum(one_hot * mix_weights[:, :, None], axis=1)

    upper = doubled(upper_rows, "expert", skip=1)
    lower = doubled(lower_rows, "expert", skip=1)
    kept = {0: [kept_rows], 1: [swapped(kept_rows, "expert", 1)]}
    given = {0: [given_rows], 1: [swapped(given_rows, "expert", 1)]}
    for slot in range(2, experts):
        kept[slot] = [upper[slot], lower[slot]]
        given[slot] = [swapped(upper[slot], "pair", 1), swapped(lower[slot], "pair", 1)]
    total = residual
    for slot in range(experts):
        kept_out, given_out = expert_parts(kept[slot], given[slot], up_held, down_held)
        received = swapped(given_out, "pair", 1)
        summed = (kept_out.astype(jnp.float32) + received.astype(jnp.float32)).astype(jnp.bfloat16)
        if slot:
            summed = swapped(summed, "expert", slot)
        column = jnp.sum(spread_mix * slot_here[slot], axis=1, keepdims=True)
        total = total + column * summed.astype(jnp.float32)
    layer_out = total.astype(jnp.bfloat16)
    stages, sides = lax.axis_size("pipe"), lax.axis_size("pair")

    def to_next(flip):
        pairs = [
            (stage * sides + place, (stage + 1) % stages * sides + (place ^ flip))
            for stage in range(stages)
            for place in range(sides)
        ]
        return lax.ppermute(layer_out, ("pipe", "pair"), pairs)

    crossed, straight = to_next(1), to_next(0)
    first = jnp.where(side == 0, straight, crossed)
    second = jnp.where(side == 0, crossed, straight)
    return jnp.concatenate([first, second], axis=0)


def local(
    tokens, expert_ids, block_mask, attn_gain, w_qkv, w_out, moe_gain, w_router, w_up, w_down
):
    rows_here = tokens.shape[0]
    experts = lax.axis_size("expert")
    capacity = min(rows_here, 2 * rows_here * expert_ids.shape[1] // experts)
    gathers = capacity == rows_here and lax.axis_size("pair") == 2 and experts & (experts - 1) == 0
    step = gathered if gathers else dispatched
    return step(
        tokens, expert_ids, block_mask, attn_gain, w_qkv, w_out, moe_gain, w_router, w_up, w_down
    )


def solution(mesh):
    return jax.shard_map(
        local,
        mesh=mesh,
        in_specs=(
            P(("pipe", "expert"), None),
            P(("pipe", "expert"), None),
            P(("pipe", "expert"), None),
            P("pipe", None),
            P("pipe", None, "pair", None),
            P("pipe", "pair", None, None),
            P("pipe", None),
            P("pipe", None, None),
            P("pipe", "expert", None, "pair"),
            P("pipe", "expert", "pair", None),
        ),
        out_specs=P(("pipe", "expert"), None),
        check_vma=False,
    )
```
